32 devices in a mesh: ctx: 4 (over x, core), wsh: 8 (over z, y).
Axes of the slice: x: 2, y: 2, z: 4, core: 2. Of those that a mesh axis runs over, the one named last changes fastest.
Arguments:
- layer_input: bfloat16 [16, 512, 1088], P('wsh', 'ctx'), may hold values from -6 to 6
- segment_ids: int32 [16, 512], P('wsh'), may hold values from 0 to 3, never falling along the last dimension, each value on 1 to 256 neighbouring positions
- block_order: int32 [8], replicated, may hold values from 0 to 7, each once
- first_gain: bfloat16 [1088], P('wsh'), may hold values from 0.25 to 1.75
- first_shift: bfloat16 [1088], P('wsh'), may hold values from -1.796875 to 1.796875
- qkv_weight: bfloat16 [1088, 3264], P('wsh'), may hold values from -0.25 to 0.25
- query_value_bias: bfloat16 [2, 1088], P(None, 'wsh'), may hold values from -1.796875 to 1.796875
- output_weight: bfloat16 [1088, 1088], P('wsh'), may hold values from -0.75 to 0.75
- output_bias: bfloat16 [1088], P('wsh'), may hold values from -1.796875 to 1.796875
- second_gain: bfloat16 [1088], P('wsh'), may hold values from 0.25 to 1.75
- second_shift: bfloat16 [1088], P('wsh'), may hold values from -1.796875 to 1.796875
- up_weight: bfloat16 [1088, 4352], P('wsh'), may hold values from -0.1875 to 0.1875
- up_bias: bfloat16 [4352], P('wsh'), may hold values from -1.796875 to 1.796875
- down_weight: bfloat16 [4352, 1088], P('wsh'), may hold values from -0.09375 to 0.09375
- down_bias: bfloat16 [1088], P('wsh'), may hold values from -1.796875 to 1.796875
- output_cotangent: bfloat16 [16, 512, 1088], P('wsh', 'ctx'), may hold values from -6 to 6
Outputs:
- layer_out: bfloat16 [16, 512, 1088], P('wsh', 'ctx')
- input_grad: bfloat16 [16, 512, 1088], P('wsh', 'ctx')
- first_gain_grad: float32 [1088], P('wsh')
- first_shift_grad: float32 [1088], P('wsh')
- qkv_weight_grad: float32 [1088, 3264], P('wsh')
- query_value_bias_grad: float32 [2, 1088], P(None, 'wsh')
- output_weight_grad: float32 [1088, 1088], P('wsh')
- output_bias_grad: float32 [1088], P('wsh')
- second_gain_grad: float32 [1088], P('wsh')
- second_shift_grad: float32 [1088], P('wsh')
- up_weight_grad: float32 [1088, 4352], P('wsh')
- up_bias_grad: float32 [4352], P('wsh')
- down_weight_grad: float32 [4352, 1088], P('wsh')
- down_bias_grad: float32 [1088], P('wsh')
The draws below stay inside these ranges and needn't reach their ends.
Inputs may be any that keep to these rules, and one draw needn't show every extreme that they name: `segment_ids`: segment numbers never fall along a sequence; a segment holds at most 256 tokens. `block_order`: each storage block number appears once.
All inputs are finite; a program needn't handle non-finite values.
Results may differ from the reference program's by a relative error of at most 0.015.
Values may be sent and summed in bfloat16 or wider, within the bound.
No kernel may reach another device: no remote copies, remote signals or barrier semaphores. Data moves between devices by JAX's collectives and lax.ppermute only.
A program may use at most 192 MiB of HBM per device.

```python
import math
import jax
import jax.numpy as jnp
import numpy as np
from jax import lax

D = 1088
FF = 4352
HEADS = 17
HEAD_DIM = 64
LEN_DEV = 128
SEQS = 16
LEN = 512
DOCS = 4
MOST = 256
N_CTX = 4


def steps_of(own_key, dims, shards, least, largest):
    loudness = 1.0
    for axis_at, shards_of in shards:
        draws = jax.random.uniform(jax.random.fold_in(jax.random.fold_in(own_key, 6), axis_at), (shards_of,), jnp.float32, least / len(shards), largest / len(shards))
        loudness = loudness * jnp.repeat(jnp.exp(draws), dims[axis_at] // shards_of).reshape((-1,) + (1,) * (len(dims) - 1 - axis_at))
    return loudness


def split_up(count, total, limit, slope):
    weights = [(1 << 20) // math.isqrt(rank ** slope) + 1 for rank in range(2, count + 1)]
    spare, holding = total - limit - (count - 1), [1] * (count - 1)
    while spare > 0:
        movable = [i for i in range(count - 1) if holding[i] < limit]
        pool, left = sum([weights[i] for i in movable]), spare
        for i in movable:
            extra = min(limit - holding[i], max(1, left * weights[i] // pool), spare)
            holding[i] = holding[i] + extra
            spare = spare - extra
    return np.array([limit] + holding)


def uneven(key, number_of, total, limit, slope):
    if number_of == 2:
        one = jax.random.randint(key, (), max(1, total - limit), min(limit, total - 1) + 1)
        return jnp.stack([one, total - one])
    sizes = jnp.asarray(split_up(number_of, total, limit, slope), jnp.int32)
    pairs = (number_of - 1) // 2
    source_of, taker = sizes[1:1 + 2 * pairs:2], sizes[2:2 + 2 * pairs:2]
    margin = jnp.minimum(source_of - 1, limit - taker)
    moved = jax.random.randint(jax.random.fold_in(key, 1), (pairs,), 0, 1 << 20) % (margin + 1)
    sizes = sizes.at[1:1 + 2 * pairs:2].set(source_of - moved).at[2:2 + 2 * pairs:2].set(taker + moved)
    return sizes[jax.random.permutation(jax.random.fold_in(key, 2), number_of)]


def noise(stream_key, dims, deviation, limit, cuts=(), held_as=jnp.bfloat16):
    values = jax.random.normal(stream_key, dims, jnp.float32) * deviation
    if len(cuts) > 0:
        values = steps_of(stream_key, dims, cuts, -0.22, 0.18) * values
    return jnp.clip(values, min=-limit, max=limit).astype(held_as)


def setup_inputs(seed: int = 0) -> dict:
    streams_of = jax.random.split(jax.random.key(seed), 17)
    return {
        "layer_input": noise(streams_of[0], (SEQS, LEN, D), 1.0, 6.0, ((0, 8), (1, 4))),
        "segment_ids": jax.vmap(lambda own: jnp.searchsorted(jnp.cumsum(uneven(own, DOCS, LEN, MOST, 2)), jnp.arange(LEN), side="right"))(jax.random.split(streams_of[1], SEQS)).reshape((SEQS, LEN)).astype(jnp.int32),
        "block_order": jax.random.permutation(streams_of[2], 2 * N_CTX).astype(jnp.int32),
        "first_gain": jnp.clip(1.0 + 0.15 * jax.random.normal(streams_of[3], (D,), jnp.float32), 0.25, 1.75).astype(jnp.bfloat16),
        "first_shift": noise(streams_of[4], (D,), 0.3, 1.796875, ((0, 8),)),
        "qkv_weight": noise(streams_of[5], (D, 3 * D), (D // 2) ** -0.5, 0.25, ((0, 8),)),
        "query_value_bias": noise(streams_of[6], (2, D), 0.3, 1.796875, ((1, 8),)),
        "output_weight": noise(streams_of[7], (D, D), (D // 16) ** -0.5, 0.75, ((0, 8),)),
        "output_bias": noise(streams_of[8], (D,), 0.3, 1.796875, ((0, 8),)),
        "second_gain": jnp.clip(1.0 + 0.15 * jax.random.normal(streams_of[9], (D,), jnp.float32), 0.25, 1.75).astype(jnp.bfloat16),
        "second_shift": noise(streams_of[10], (D,), 0.3, 1.796875, ((0, 8),)),
        "up_weight": noise(streams_of[11], (D, FF), D ** -0.5, 0.1875, ((0, 8),)),
        "up_bias": noise(streams_of[12], (FF,), 0.3, 1.796875, ((0, 8),)),
        "down_weight": noise(streams_of[13], (FF, D), FF ** -0.5, 0.09375, ((0, 8),)),
        "down_bias": noise(streams_of[14], (D,), 0.3, 1.796875, ((0, 8),)),
        "output_cotangent": noise(streams_of[15], (SEQS, LEN, D), 1.0, 6.0, ((0, 8), (1, 4))),
    }


EPSILON = 1e-05
NEG_FILL = -1e+30

@jax.custom_vjp
def low(v):
    return lax.optimization_barrier(v.astype(jnp.bfloat16)).astype(jnp.float32)

@jax.custom_vjp
def low_back(v):
    return v

def low_keep(v):
    return (low(v), None)

def low_pass(kept, grad):
    return (grad,)

def back_keep(v):
    return (v, None)

def back_low(kept, grad):
    return (low(grad),)
low.defvjp(low_keep, low_pass)
low_back.defvjp(back_keep, back_low)

def matmul_high(left, right):
    return jnp.dot(left, right, precision=lax.Precision.HIGHEST)

def norm_rows(values, gain, offset):
    average = lax.optimization_barrier(jnp.mean(values, axis=-1, keepdims=True))
    centered = values - average
    variance = lax.optimization_barrier(jnp.mean(centered * centered, axis=-1, keepdims=True))
    return centered * lax.rsqrt(variance + EPSILON) * gain + offset

def attend_block(query_rows, query_pos, query_seg, keys, values, key_pos, key_seg):
    scaling = HEAD_DIM ** (-0.5)
    raw_scores = jnp.einsum('qhd,khd->hqk', query_rows, keys, precision=lax.Precision.HIGHEST) * scaling
    scores = low_back(raw_scores)
    allowed = (query_seg[:, None] == key_seg[None, :]) & (key_pos[None, :] <= query_pos[:, None])
    weights = low(jax.nn.softmax(jnp.where(allowed[None], scores, NEG_FILL), axis=-1))
    return jnp.einsum('hqk,khd->qhd', weights, values, precision=lax.Precision.HIGHEST)

def attend_sequence(packed, positions):
    per_seq, seq_segs = packed
    queries = per_seq[:, 0]
    keys = per_seq[:, 1]
    values = per_seq[:, 2]
    block_rows = math.gcd(LEN, 512)
    count_blocks = LEN // block_rows
    checked = jax.checkpoint(attend_block)

    def one_block(stacked):
        query_rows, query_pos, query_seg = stacked
        return checked(query_rows, query_pos, query_seg, keys, values, positions, seq_segs)
    blocked = (queries.reshape(count_blocks, block_rows, HEADS, HEAD_DIM), positions.reshape(count_blocks, block_rows), seq_segs.reshape(count_blocks, block_rows))
    return lax.map(one_block, blocked).reshape(LEN, HEADS, HEAD_DIM)

def forward(layer_input, first_gain, first_shift, qkv_weight, query_value_bias, output_weight, output_bias, second_gain, second_shift, up_weight, up_bias, down_weight, down_bias, key_segs, positions):
    input_rows = layer_input.reshape(SEQS * LEN, D)
    first_in = low(norm_rows(input_rows, first_gain, first_shift))
    full_bias = jnp.concatenate([query_value_bias[0], jnp.zeros((D,), jnp.float32), query_value_bias[1]])
    projected = low(low_back(matmul_high(first_in, qkv_weight) + full_bias))
    per_seq = projected.reshape(SEQS, LEN, 3, HEADS, HEAD_DIM)
    attended = lax.map(lambda packed: attend_sequence(packed, positions), (per_seq, key_segs))
    attended = low(low_back(attended.reshape(SEQS * LEN, D)))
    branch = low_back(matmul_high(attended, output_weight) + output_bias)
    resid = input_rows + branch
    second_in = low(norm_rows(resid, second_gain, second_shift))
    hidden = low_back(matmul_high(second_in, up_weight) + up_bias)
    activated = low(jax.nn.gelu(hidden, approximate=False))
    result = resid + matmul_high(activated, down_weight) + down_bias
    return result.reshape(SEQS, LEN, D)

def reference(layer_input, segment_ids, block_order, first_gain, first_shift, qkv_weight, query_value_bias, output_weight, output_bias, second_gain, second_shift, up_weight, up_bias, down_weight, down_bias, output_cotangent):
    half_block = LEN_DEV // 2
    row_ids = jnp.arange(LEN, dtype=jnp.int32)
    positions = (block_order[row_ids // half_block] * half_block + row_ids % half_block).astype(jnp.int32)
    key_segs = jnp.take(segment_ids, positions, axis=1)
    float_args = tuple((argument.astype(jnp.float32) for argument in (layer_input, first_gain, first_shift, qkv_weight, query_value_bias, output_weight, output_bias, second_gain, second_shift, up_weight, up_bias, down_weight, down_bias)))

    def wrapped(*params):
        return forward(*params, key_segs, positions)
    result, pullback = jax.vjp(wrapped, *float_args)
    gradients = pullback(output_cotangent.astype(jnp.float32))
    return (result.astype(jnp.bfloat16), gradients[0].astype(jnp.bfloat16), gradients[1], gradients[2], gradients[3], gradients[4], gradients[5], gradients[6], gradients[7], gradients[8], gradients[9], gradients[10], gradients[11], gradients[12])
```

```python
import functools

import jax
import jax.numpy as jnp
import numpy as np
from jax import lax
from jax.experimental import pallas as pl
from jax.experimental.pallas import tpu as pltpu
from jax.sharding import PartitionSpec as P

HEADS = 17
HEAD_DIM = 64

EPSILON = 1e-05
NEG_FILL = -1e30
SCALING = HEAD_DIM ** (-0.5)
F32 = jnp.float32
BF16 = jnp.bfloat16
LANES = 128
VECTORS = 8


def reverse_bits(value, size):
    out = 0
    bit = 1
    while bit < size:
        out = out * 2 + (1 if value & bit else 0)
        bit *= 2
    return out


def up_to_lanes(count):
    return -(-count // LANES) * LANES


def flip(block, size, bit):
    return lax.ppermute(block, "ctx", [(i, i ^ bit) for i in range(size)])


def ctx_gather(block, size):
    stacked = block[None]
    bit = size // 2
    while bit:
        stacked = jnp.concatenate([stacked, flip(stacked, size, bit)], axis=0)
        bit //= 2
    return stacked


def add_low(kept, arrived):
    return kept.astype(F32) + arrived.astype(F32)


def fold(parts, size, last):
    bit = 1
    while bit < last:
        half = parts.shape[0] // 2
        parts = add_low(parts[:half], flip(parts[half:].astype(BF16), size, bit))
        bit *= 2
    return parts[0]


def ring_order(size):
    return list(range(0, size, 2)) + list(range(size - 1, 0, -2))


def ring_routes(size):
    order = ring_order(size)
    ahead = [(order[i], order[(i + 1) % size]) for i in range(size)]
    return ahead, [(b, a) for a, b in ahead]


def scalar_table(ctx, wsh):
    order = ring_order(wsh)
    table = np.zeros((ctx, wsh, 2 + wsh), np.int32)
    for c in range(ctx):
        for w in range(wsh):
            at = order.index(w)
            ahead = [order[(at + d) % wsh] for d in range(wsh)]
            table[c, w] = [c, reverse_bits(c, ctx)] + ahead
    return table


def reach(size, long_ahead):
    ups, downs = size // 2, size - 1 - size // 2
    return (ups, downs) if long_ahead else (downs, ups)


def ring_gather(piece, size, long_ahead):
    ahead, behind = ring_routes(size)
    ups, downs = reach(size, long_ahead)
    pieces, distances = [piece], [0]
    forward = backward = piece
    for step in range(1, max(ups, downs) + 1):
        if step <= ups:
            forward = lax.ppermute(forward, "wsh", ahead)
            pieces.append(forward)
            distances.append(size - step)
        if step <= downs:
            backward = lax.ppermute(backward, "wsh", behind)
            pieces.append(backward)
            distances.append(step)
    return pieces, distances


def ring_scatter(step_sum, size, long_ahead):
    ahead, behind = ring_routes(size)
    ups, downs = reach(size, long_ahead)
    forward, backward = [], []
    for step in range(max(ups, downs), 0, -1):
        if step <= ups:
            forward = [lax.ppermute(step_sum(step, forward), "wsh", ahead)]
        if step <= downs:
            backward = [lax.ppermute(step_sum(size - step, backward), "wsh", behind)]
    return step_sum(0, forward + backward)


def dot_rows(left, right):
    return lax.dot_general(left, right, (((1,), (1,)), ((), ())), preferred_element_type=F32)


def dot_cols(left, right):
    return lax.dot_general(left, right, (((0,), (0,)), ((), ())), preferred_element_type=F32)


def dot(left, right):
    return jnp.dot(left, right, preferred_element_type=F32)


def normalize(rows):
    centered = rows - jnp.mean(rows, axis=-1, keepdims=True)
    variance = jnp.mean(centered * centered, axis=-1, keepdims=True)
    scale = lax.rsqrt(variance + EPSILON)
    return centered * scale, scale


def norm_back(grad, normed, scale):
    return scale * (
        grad
        - jnp.mean(grad, axis=-1, keepdims=True)
        - normed * jnp.mean(grad * normed, axis=-1, keepdims=True)
    )


def whole_spec(shape):
    return pl.BlockSpec(shape, lambda *a: (0,) * len(shape), pipeline_mode=pl.Buffered(1))


def call(kernel, grid, in_specs, out_specs, out_shape, scalars, args, name, scratch=(), aliases=None, cost=None):
    return pl.pallas_call(
        kernel,
        grid_spec=pltpu.PrefetchScalarGridSpec(
            num_scalar_prefetch=1,
            grid=grid,
            in_specs=in_specs,
            out_specs=out_specs,
            scratch_shapes=list(scratch),
        ),
        out_shape=out_shape,
        input_output_aliases=aliases or {},
        compiler_params=pltpu.CompilerParams(vmem_limit_bytes=60 << 20),
        cost_estimate=cost,
        name=name,
    )(scalars, *args)


def shape_of(dims, dtype):
    return jax.ShapeDtypeStruct(tuple(dims), dtype)


def cost(flops, moved):
    return pl.CostEstimate(flops=int(flops), bytes_accessed=int(moved), transcendentals=0)


def for_each(value, count, body):
    for c in range(count):
        pl.when(value == c)(functools.partial(body, c))


class Plan:
    def __init__(self, layer_input, qkv_weight, down_weight, ctx, wsh):
        self.ctx, self.wsh = ctx, wsh
        self.seqs, self.rows, self.width = layer_input.shape
        self.shard = qkv_weight.shape[0]
        self.hidden = down_weight.shape[0]
        self.units = self.hidden // ctx
        self.ffn = self.units * wsh
        self.own = self.seqs * self.rows
        self.heads = -(-HEADS // ctx)
        self.starts = [(c * HEADS) // ctx for c in range(ctx + 1)]
        self.counts = [self.starts[c + 1] - self.starts[c] for c in range(ctx)]
        self.span = self.heads * HEAD_DIM
        self.vec_at = 3 * self.span
        self.out_at = up_to_lanes(self.vec_at + VECTORS)
        self.first_wide = self.out_at + self.span
        self.down_at = up_to_lanes(self.ffn)
        self.bias_at = self.down_at + self.width
        self.rings = self.shard % 8 == 0 and self.units == self.shard


def slice_kernel(plan, sc, qkv_ref, out_ref, vec_ref, piece_ref):
    span, width = plan.span, plan.width

    def body(c):
        first = plan.starts[c] * HEAD_DIM
        for part in range(3):
            piece_ref[:, part * span : (part + 1) * span] = qkv_ref[
                :, part * width + first : part * width + first + span
            ]
        piece_ref[:, plan.out_at : plan.out_at + span] = out_ref[:, first : first + span]

    for_each(sc[0], plan.ctx, body)
    turned = vec_ref[...].T
    piece_ref[:, plan.vec_at : plan.vec_at + VECTORS] = turned[:, :VECTORS].astype(BF16)


def slice_up_kernel(plan, sc, up_ref, piece_ref):
    units, ctx = plan.units, plan.ctx

    def body(c):
        for w in range(plan.wsh):
            at = (w * ctx + c) * units
            piece_ref[:, w * units : (w + 1) * units] = up_ref[:, at : at + units]

    for_each(sc[0], ctx, body)


def assemble(sc, distances, pieces, wide, rows):
    if len(pieces) == 1:
        wide[...] = pieces[0][...].astype(F32)
    else:
        for piece, distance in zip(pieces, distances, strict=True):
            at = pl.multiple_of(sc[2 + distance] * rows, 8)
            wide[pl.ds(at, rows), :] = piece[...].astype(F32)


def project_kernel(plan, distances, sc, x_ref, *refs):
    count = len(distances)
    pieces = refs[:count]
    first_ref, proj_ref, qkv_ref, out_ref, vec_ref, wide, bias = refs[count:]
    span = plan.span

    @pl.when(pl.program_id(0) == 0)
    def _():
        assemble(sc, distances, pieces, wide, plan.shard)
        qkv_ref[...] = wide[:, : 3 * span].astype(BF16)
        out_ref[...] = wide[:, plan.out_at :].astype(BF16)
        aligned = plan.vec_at // LANES * LANES
        turned = wide[:, aligned : aligned + LANES].T
        vec_ref[...] = turned[plan.vec_at - aligned : plan.vec_at - aligned + VECTORS]

        def body(c):
            first = plan.starts[c] * HEAD_DIM
            bias[:, :span] = vec_ref[2:3, first : first + span]
            bias[:, span : 2 * span] = jnp.zeros((1, span), F32)
            bias[:, 2 * span :] = vec_ref[3:4, first : first + span]

        for_each(sc[0], plan.ctx, body)

    normed, _ = normalize(x_ref[...].reshape(plan.own, plan.width).astype(F32))
    first_in = (normed * vec_ref[0:1] + vec_ref[1:2]).astype(BF16)
    first_ref[...] = first_in
    proj = (dot(first_in, qkv_ref[...]) + bias[...]).astype(BF16)
    proj_ref[...] = proj.reshape(proj_ref.shape)


def project(plan, sc, x, pieces, distances):
    ctx, own, width, span = plan.ctx, plan.own, plan.width, plan.span
    tile = (1, plan.seqs, plan.rows)
    return call(
        functools.partial(project_kernel, plan, distances),
        (ctx,),
        [pl.BlockSpec(tile + (width,), lambda p, sc: (p, 0, 0, 0))]
        + [whole_spec(piece.shape) for piece in pieces],
        [
            pl.BlockSpec((own, width), lambda p, sc: (p, 0)),
            pl.BlockSpec(tile + (3 * span,), lambda p, sc: (p, 0, 0, 0)),
            whole_spec((width, 3 * span)),
            whole_spec((width, span)),
            whole_spec((VECTORS, width)),
        ],
        [
            shape_of((ctx * own, width), BF16),
            shape_of((ctx, plan.seqs, plan.rows, 3 * span), BF16),
            shape_of((width, 3 * span), BF16),
            shape_of((width, span), BF16),
            shape_of((VECTORS, width), F32),
        ],
        sc,
        [x] + pieces,
        "project",
        [pltpu.VMEM((width, plan.first_wide), F32), pltpu.VMEM((1, 3 * span), F32)],
        cost=cost(2 * ctx * own * width * 3 * span, 12 << 20),
    )


def attend_kernel(heads, qpos, qseg, kpos, kseg, q_ref, kv_ref, out_ref, weight_ref):
    bq = q_ref.shape[0] * q_ref.shape[2]
    length = kv_ref.shape[0] * kv_ref.shape[2]
    allowed = (qseg[0] == kseg[0]) & (kpos[...] <= qpos[...])
    bias = jnp.where(allowed, 0.0, NEG_FILL)
    outs = []
    for h in range(heads):
        lanes = [pl.ds((part * heads + h) * HEAD_DIM, HEAD_DIM) for part in range(3)]
        q = q_ref[:, 0, :, lanes[0]].reshape(bq, HEAD_DIM) * jnp.asarray(SCALING, BF16)
        k = kv_ref[:, 0, :, lanes[1]].reshape(length, HEAD_DIM)
        v = kv_ref[:, 0, :, lanes[2]].reshape(length, HEAD_DIM)
        scores = dot_rows(q, k) + bias
        top = jnp.max(scores, axis=-1, keepdims=True)
        grown = jnp.exp(scores - top)
        total = jnp.sum(grown, axis=-1, keepdims=True)
        weights = (grown * (1.0 / total)).astype(BF16)
        weight_ref[0, h] = weights
        outs.append(dot(weights, v).astype(BF16))
    attended = jnp.concatenate(outs, axis=-1)
    out_ref[:, 0] = attended.reshape(out_ref.shape[0], out_ref.shape[2], attended.shape[-1])


def attend(plan, projected, pos, seg):
    slots, seqs, rows, wide = projected.shape
    heads, span = plan.heads, plan.span
    length = slots * rows
    take = min(slots, 4)
    bq = take * rows
    return pl.pallas_call(
        functools.partial(attend_kernel, heads),
        grid=(seqs, slots // take),
        in_specs=[
            pl.BlockSpec((bq, 1), lambda s, b: (b, 0)),
            pl.BlockSpec((1, bq, 1), lambda s, b: (s, b, 0)),
            pl.BlockSpec((1, length), lambda s, b: (0, 0)),
            pl.BlockSpec((1, 1, length), lambda s, b: (s, 0, 0)),
            pl.BlockSpec((take, 1, rows, wide), lambda s, b: (b, s, 0, 0)),
            pl.BlockSpec((slots, 1, rows, wide), lambda s, b: (0, s, 0, 0)),
        ],
        out_specs=[
            pl.BlockSpec((take, 1, rows, span), lambda s, b: (b, s, 0, 0)),
            pl.BlockSpec((1, heads, bq, length), lambda s, b: (s, 0, b, 0)),
        ],
        out_shape=[
            shape_of((slots, seqs, rows, span), BF16),
            shape_of((seqs, heads, length, length), BF16),
        ],
        compiler_params=pltpu.CompilerParams(vmem_limit_bytes=60 << 20),
        cost_estimate=cost(16 * seqs * heads * length * length * HEAD_DIM, 16 << 20),
        name="attend",
    )(pos[:, None], seg[:, :, None], pos[None], seg[:, None], projected, projected)


def feed_kernel(plan, parity, up_distances, down_distances, sc, x_ref, cot_ref, vec_ref, *refs):
    ctx, width, span, own = plan.ctx, plan.width, plan.span, plan.own
    refs = list(refs)
    atts = [refs.pop(0) for _ in range(ctx)]
    outs = ups = downs = ()
    if parity:
        outs = [refs.pop(0) for _ in range(ctx)]
        ups = [refs.pop(0) for _ in up_distances]
        downs = [refs.pop(0) for _ in down_distances]
        part_ref, back_ref, act_ref, grad_ref, second_ref, att_ref, sums_ref, bias_sums = refs[:8]
        out_w, up_w, down_w, bias_w, wide, wide_down = refs[8:]
    else:
        out_w, up_w, down_w, bias_w = refs[:4]
        part_ref, back_ref, act_ref, grad_ref, second_ref, att_ref, sums_ref, bias_sums = refs[8:16]
        resid_ref = refs[16]
    turn = pl.program_id(0)

    @pl.when(turn == 0)
    def _():
        sums_ref[...] = jnp.zeros_like(sums_ref)
        bias_sums[...] = jnp.zeros_like(bias_sums)
        if parity:
            for c in range(ctx):
                out_w[:, plan.starts[c] * HEAD_DIM : plan.starts[c + 1] * HEAD_DIM] = outs[c][
                    0, :, : plan.counts[c] * HEAD_DIM
                ]
            assemble(sc, up_distances, ups, wide, plan.shard)
            up_w[...] = wide[...].astype(BF16)
            assemble(sc, down_distances, downs, wide_down, plan.units)
            down_w[...] = wide_down[:, :width].astype(BF16)
            aligned = width // LANES * LANES
            turned = wide_down[:, aligned:].T
            bias_w[...] = turned[width - aligned : width - aligned + 1]

    attended = jnp.concatenate(
        [atts[c][0, 0, :, :, : plan.counts[c] * HEAD_DIM] for c in range(ctx)], axis=-1
    ).reshape(own, width)
    att_ref[0] = attended
    resid = x_ref[...].reshape(own, width).astype(F32) + (dot(attended, out_w[...]) + vec_ref[4:5])
    if not parity:

        @pl.when(turn == 0)
        def _():
            resid_ref[...] = resid

    normed, _ = normalize(resid)
    second_in = (normed * vec_ref[5:6] + vec_ref[6:7]).astype(BF16)
    second_ref[0] = second_in
    hidden = dot(second_in, up_w[...]) + bias_w[...]
    phi = 0.5 * (1.0 + lax.erf(hidden * (2.0**-0.5)))
    slope = phi + hidden * jnp.exp(-0.5 * hidden * hidden) * 0.3989422804014327
    activated = (hidden * phi).astype(BF16)
    act_ref[0] = activated
    part_ref[0] = dot(activated, down_w[...]).astype(BF16)
    cot = cot_ref[...].reshape(own, width)
    up_grad = (slope * dot_rows(cot, down_w[...])).astype(BF16)
    grad_ref[0] = up_grad
    back = dot_rows(up_grad, up_w[...])
    back_ref[0] = back.astype(BF16)
    sums_ref[0:1] += jnp.sum(back * normed, axis=0, keepdims=True)
    sums_ref[1:2] += jnp.sum(back, axis=0, keepdims=True)
    bias_sums[...] += jnp.sum(up_grad.astype(F32), axis=0, keepdims=True)


def feed(plan, sc, parity, x, cot, vec, att, weights, kept):
    ctx, own, width, ffn, span = plan.ctx, plan.own, plan.width, plan.ffn, plan.span
    tile = (1, plan.seqs, plan.rows)
    token_spec = pl.BlockSpec(tile + (width,), lambda t, sc: (2 * t + parity, 0, 0, 0))

    def att_spec(c):
        place = reverse_bits(c, ctx)
        return pl.BlockSpec(
            (1,) + tile + (span,),
            lambda t, sc: (place ^ sc[1], (2 * t + parity) ^ place ^ sc[1], 0, 0, 0),
        )

    def out_spec(c):
        place = reverse_bits(c, ctx)
        return pl.BlockSpec(
            (1, width, span), lambda t, sc: (place ^ sc[1], 0, 0), pipeline_mode=pl.Buffered(1)
        )

    in_specs = [token_spec, token_spec, whole_spec(vec.shape)] + [att_spec(c) for c in range(ctx)]
    args = [x, cot, vec] + [att] * ctx
    half = [(ctx // 2, own, width), (ctx // 2, own, width)]
    full = [(ctx, own, ffn), (ctx, own, ffn), (ctx, own, width), (ctx, own, width)]
    sums = [(VECTORS, width), (1, ffn)]
    out_shape = (
        [shape_of(s, BF16) for s in half + full] + [shape_of(s, F32) for s in sums]
    )
    out_specs = [pl.BlockSpec((1, own, width), lambda t, sc: (t, 0, 0))] * 2 + [
        pl.BlockSpec((1,) + s[1:], lambda t, sc: (2 * t + parity, 0, 0)) for s in full
    ]
    out_specs += [whole_spec(s) for s in sums]
    scratch = []
    aliases = {}
    up_distances = down_distances = None
    if parity:
        outs, ups, up_distances, downs, down_distances = weights
        in_specs += [out_spec(c) for c in range(ctx)]
        in_specs += [whole_spec(piece.shape) for piece in ups + downs]
        args += [outs] * ctx + ups + downs
        made = [(width, width), (width, ffn), (ffn, width), (1, ffn)]
        out_shape += [shape_of(s, BF16 if s[0] > 1 else F32) for s in made]
        out_specs += [whole_spec(s) for s in made]
        scratch = [
            pltpu.VMEM((width, ffn), F32),
            pltpu.VMEM((ffn, up_to_lanes(width + 1)), F32),
        ]
    else:
        in_specs += [whole_spec(w.shape) for w in weights]
        args += list(weights)
        aliases = {1 + len(args) + i: 2 + i for i in range(4)}
        in_specs += [pl.BlockSpec(memory_space=pl.ANY)] * 4
        args += list(kept)
        out_shape += [shape_of((own, width), F32)]
        out_specs += [whole_spec((own, width))]
    return call(
        functools.partial(feed_kernel, plan, parity, up_distances, down_distances),
        (ctx // 2,),
        in_specs,
        out_specs,
        out_shape,
        sc,
        args,
        "feed_odd" if parity else "feed_even",
        scratch,
        aliases,
        cost(ctx * own * width * (width + 4 * ffn), 24 << 20),
    )


def second_kernel(plan, sc, even_ref, odd_ref, cot_ref, resid_ref, vec_ref, branch_ref, grad_ref, sums_ref):
    @pl.when(pl.program_id(0) == 0)
    def _():
        sums_ref[...] = jnp.zeros_like(sums_ref)

    back = even_ref[...] + odd_ref[...].astype(F32)
    normed, scale = normalize(resid_ref[...])
    cot = cot_ref[...].astype(F32)
    grad = cot + norm_back(back * vec_ref[5:6], normed, scale)
    low = grad.astype(BF16)
    branch_ref[...] = low
    grad_ref[...] = grad
    sums_ref[0:1] += jnp.sum(low.astype(F32), axis=0, keepdims=True)
    sums_ref[1:2] += jnp.sum(cot, axis=0, keepdims=True)


def own_blocks(plan, kernel, sc, args, whole, outs, sums, name):
    block = pl.BlockSpec((plan.rows, plan.width), lambda t, sc: (t, 0))
    return call(
        kernel,
        (plan.seqs,),
        [block] * len(args) + [whole_spec(w.shape) for w in whole],
        [block] * len(outs) + [whole_spec(s) for s in sums],
        [shape_of((plan.own, plan.width), d) for d in outs] + [shape_of(s, F32) for s in sums],
        sc,
        list(args) + list(whole),
        name,
        cost=cost(40 * plan.own * plan.width, 4 << 20),
    )


def first_kernel(plan, sc, kept_ref, arrived_ref, x_ref, resid_grad_ref, vec_ref, out_ref):
    back = kept_ref[...] + arrived_ref[...].astype(F32)
    normed, scale = normalize(x_ref[...].astype(F32))
    out_ref[...] = (
        resid_grad_ref[...] + norm_back(back * vec_ref[0:1], normed, scale)
    ).astype(BF16)


def attend_back_kernel(plan, blocks, sc, q_ref, kv_ref, weight_ref, branch_ref, wo_ref, out_ref, dk_acc, dv_acc):
    heads, span = plan.heads, plan.span
    slots, rows = q_ref.shape[0], q_ref.shape[2]
    bq = slots * rows
    length = kv_ref.shape[0] * rows
    turn = pl.program_id(1)
    first = (sc[0] * HEADS) // plan.ctx
    owned = ((sc[0] + 1) * HEADS) // plan.ctx - first
    wo = wo_ref[pl.ds(pl.multiple_of(first * HEAD_DIM, HEAD_DIM), span), :]
    all_grads = dot_rows(branch_ref[...].reshape(bq, plan.width), wo)
    lane = lax.broadcasted_iota(jnp.int32, all_grads.shape, 1)
    all_grads = jnp.where(lane < owned * HEAD_DIM, all_grads, 0.0).astype(BF16)
    for h in range(heads):
        lanes = [pl.ds((part * heads + h) * HEAD_DIM, HEAD_DIM) for part in range(3)]
        q = q_ref[:, 0, :, lanes[0]].reshape(bq, HEAD_DIM) * jnp.asarray(SCALING, BF16)
        k = kv_ref[:, 0, :, lanes[1]].reshape(length, HEAD_DIM)
        v = kv_ref[:, 0, :, lanes[2]].reshape(length, HEAD_DIM)
        grad = all_grads[:, h * HEAD_DIM : (h + 1) * HEAD_DIM]
        weights = weight_ref[0, h]
        probs = weights.astype(F32)
        dprob = dot_rows(grad, v)
        delta = jnp.sum(probs * dprob, axis=-1, keepdims=True)
        score_grad = (probs * (dprob - delta)).astype(BF16)
        dq = dot(score_grad, k) * SCALING
        out_ref[pl.ds(turn * slots, slots), 0, :, lanes[0]] = dq.astype(BF16).reshape(
            slots, rows, HEAD_DIM
        )
        dk = dot_cols(q, score_grad).T
        dv = dot_cols(grad, weights).T

        def put(dk, dv):
            out_ref[:, 0, :, lanes[1]] = dk.astype(BF16).reshape(-1, rows, HEAD_DIM)
            out_ref[:, 0, :, lanes[2]] = dv.astype(BF16).reshape(-1, rows, HEAD_DIM)

        if blocks == 1:
            put(dk, dv)
        else:

            @pl.when(turn == 0)
            def _():
                dk_acc[h] = dk
                dv_acc[h] = dv

            @pl.when(turn > 0)
            def _():
                dk_acc[h] += dk
                dv_acc[h] += dv

            @pl.when(turn == blocks - 1)
            def _():
                put(dk_acc[h], dv_acc[h])


def attend_back(plan, sc, projected, weights, branch, wo):
    slots, seqs, rows, wide = projected.shape
    heads = plan.heads
    length = slots * rows
    take = min(slots, 4)
    blocks = slots // take
    bq = take * rows
    acc = (heads, length if blocks > 1 else 8, HEAD_DIM)
    return call(
        functools.partial(attend_back_kernel, plan, blocks),
        (seqs, blocks),
        [
            pl.BlockSpec((take, 1, rows, wide), lambda s, b, sc: (b, s, 0, 0)),
            pl.BlockSpec((slots, 1, rows, wide), lambda s, b, sc: (0, s, 0, 0)),
            pl.BlockSpec((1, heads, bq, length), lambda s, b, sc: (s, 0, b, 0)),
            pl.BlockSpec((take, 1, rows, plan.width), lambda s, b, sc: (b, s, 0, 0)),
            whole_spec(wo.shape),
        ],
        pl.BlockSpec((slots, 1, rows, wide), lambda s, b, sc: (0, s, 0, 0)),
        shape_of((slots, seqs, rows, wide), BF16),
        sc,
        [projected, projected, weights, branch, wo],
        "attend_back",
        [pltpu.VMEM(acc, F32), pltpu.VMEM(acc, F32)],
        cost=cost(32 * seqs * heads * length * length * HEAD_DIM, 16 << 20),
    )


def first_back_kernel(plan, sc, grad_ref, x_ref, w_ref, second_ref, odd_ref, even_ref, back_ref, small_ref, sums, cols):
    span, width = plan.span, plan.width
    turn = pl.program_id(0)

    @pl.when(turn == 0)
    def _():
        sums[...] = jnp.zeros_like(sums)
        cols[...] = jnp.zeros_like(cols)

    grad = grad_ref[...].reshape(plan.own, 3 * span)
    back = dot_rows(grad, w_ref[...])
    back_ref[0] = back.astype(BF16)
    normed, _ = normalize(x_ref[...].reshape(plan.own, width).astype(F32))
    sums[0:1, :width] += jnp.sum(back * normed, axis=0, keepdims=True)
    sums[1:2, :width] += jnp.sum(back, axis=0, keepdims=True)
    cols[...] += jnp.sum(grad.astype(F32), axis=0, keepdims=True)

    @pl.when(turn == plan.ctx - 1)
    def _():
        def body(c):
            at = plan.starts[c] * HEAD_DIM
            count = plan.counts[c] * HEAD_DIM
            sums[2:3, at : at + count] = cols[:, :count]
            sums[3:4, at : at + count] = cols[:, 2 * span : 2 * span + count]

        for_each(sc[0], plan.ctx, body)
        sums[4:5, :width] = second_ref[0:1]
        sums[5:6, :width] = odd_ref[0:1] + even_ref[0:1]
        sums[6:7, :width] = odd_ref[1:2] + even_ref[1:2]
        sums[7:8, :width] = second_ref[1:2]
        small_ref[...] = sums[...].T[:width]


def first_back(plan, sc, qkv_grad, x, qkv_full, second_sums, odd_sums, even_sums):
    ctx, own, width, span = plan.ctx, plan.own, plan.width, plan.span
    tile = (1, plan.seqs, plan.rows)
    return call(
        functools.partial(first_back_kernel, plan),
        (ctx,),
        [
            pl.BlockSpec(tile + (3 * span,), lambda p, sc: (p, 0, 0, 0)),
            pl.BlockSpec(tile + (width,), lambda p, sc: (p, 0, 0, 0)),
            whole_spec(qkv_full.shape),
        ]
        + [whole_spec(s.shape) for s in (second_sums, odd_sums, even_sums)],
        [
            pl.BlockSpec((1, own, width), lambda p, sc: (p, 0, 0)),
            whole_spec((width, LANES)),
        ],
        [shape_of((ctx, own, width), BF16), shape_of((width, LANES), F32)],
        sc,
        [qkv_grad, x, qkv_full, second_sums, odd_sums, even_sums],
        "first_back",
        [pltpu.VMEM((LANES, up_to_lanes(width)), F32), pltpu.VMEM((1, 3 * span), F32)],
        cost=cost(2 * ctx * own * width * 3 * span, 12 << 20),
    )


def step_kernel(places, sc, *refs):
    count = len(places)
    arrived, out_ref = refs[count:-1], refs[-1]
    for part, (at, wide) in zip(refs[:count], places, strict=True):
        total = part[:, :wide]
        for other in arrived:
            total = total + other[:, at : at + wide].astype(F32)
        out_ref[:, at : at + wide] = total.astype(BF16)


def step_sum(sc, parts, places, rows, wide, name, distance, arrived):
    return call(
        functools.partial(step_kernel, places),
        (1,),
        [
            pl.BlockSpec((rows, p.shape[1]), lambda i, sc: (sc[2 + distance], 0)) for p in parts
        ]
        + [whole_spec((rows, wide)) for _ in arrived],
        whole_spec((rows, wide)),
        shape_of((rows, wide), BF16),
        sc,
        list(parts) + list(arrived),
        name,
        cost=cost(1 << 20, 2 << 20),
    )


def ffn_out_kernel(plan, sc, *refs):
    pieces = refs[: plan.ctx]
    up_ref, down_ref, bias_ref = refs[plan.ctx :]
    units, ctx, width = plan.units, plan.ctx, plan.width
    for c, piece in enumerate(pieces):
        for w in range(plan.wsh):
            at = (w * ctx + c) * units
            up_ref[:, at : at + units] = piece[0, :, w * units : (w + 1) * units].astype(F32)
        down_ref[c * units : (c + 1) * units, :] = piece[
            0, :, plan.down_at : plan.down_at + width
        ].astype(F32)
        aligned = plan.bias_at // LANES * LANES
        tail = piece[0, :, aligned : plan.bias_at + 1].astype(F32)
        tail = jnp.concatenate([tail, jnp.zeros((units, LANES - tail.shape[1]), F32)], axis=1)
        at = plan.bias_at - aligned
        bias_ref[:, c * units : (c + 1) * units] = tail.T[at : at + 1]


def attn_out_kernel(plan, sc, *refs):
    pieces = refs[: plan.ctx]
    qkv_ref, out_ref, small_ref = refs[plan.ctx :]
    span, width = plan.span, plan.width
    aligned = plan.vec_at // LANES * LANES
    tails = 0.0
    for c, piece in enumerate(pieces):
        first, count = plan.starts[c] * HEAD_DIM, plan.counts[c] * HEAD_DIM
        for part in range(3):
            at = part * width + first
            qkv_ref[:, at : at + count] = piece[0, :, part * span : part * span + count].astype(F32)
        out_ref[:, first : first + count] = piece[
            0, :, plan.out_at : plan.out_at + count
        ].astype(F32)
        tails = tails + piece[0, :, aligned : aligned + LANES].astype(F32)
    small_ref[...] = tails.T[plan.vec_at - aligned : plan.vec_at - aligned + VECTORS]


def spread_out(plan, kernel, sc, gathered, outs, name):
    def spec(c):
        place = reverse_bits(c, plan.ctx)
        return pl.BlockSpec(
            (1,) + gathered.shape[1:],
            lambda i, sc: (place ^ sc[1], 0, 0),
            pipeline_mode=pl.Buffered(1),
        )

    return call(
        functools.partial(kernel, plan),
        (1,),
        [spec(c) for c in range(plan.ctx)],
        [whole_spec(s) for s in outs],
        [shape_of(s, F32) for s in outs],
        sc,
        [gathered] * plan.ctx,
        name,
        cost=cost(1 << 20, 8 << 20),
    )


def per_device(
    layer_input,
    segment_ids,
    block_order,
    first_gain,
    first_shift,
    qkv_weight,
    query_value_bias,
    output_weight,
    output_bias,
    second_gain,
    second_shift,
    up_weight,
    up_bias,
    down_weight,
    down_bias,
    output_cotangent,
):
    ctx = lax.axis_size("ctx")
    wsh = lax.axis_size("wsh")
    me = lax.axis_index("ctx")
    plan = Plan(layer_input, qkv_weight, down_weight, ctx, wsh)
    seqs, rows, width, own = plan.seqs, plan.rows, plan.width, plan.own
    shard, units, span = plan.shard, plan.units, plan.span
    half_block = rows // 2
    last = ctx // 2
    sc = lax.dynamic_slice(
        jnp.asarray(scalar_table(ctx, wsh)), (me, lax.axis_index("wsh"), 0), (1, 1, 2 + wsh)
    ).reshape(2 + wsh)

    vectors = jnp.stack(
        [
            first_gain,
            first_shift,
            query_value_bias[0],
            query_value_bias[1],
            output_bias,
            second_gain,
            second_shift,
            down_bias,
        ]
    ).astype(F32)
    first_piece = call(
        functools.partial(slice_kernel, plan),
        (1,),
        [whole_spec(a.shape) for a in (qkv_weight, output_weight, vectors)],
        whole_spec((shard, plan.first_wide)),
        shape_of((shard, plan.first_wide), BF16),
        sc,
        [qkv_weight, output_weight, vectors],
        "slice_first",
    )
    up_piece = call(
        functools.partial(slice_up_kernel, plan),
        (1,),
        [whole_spec(up_weight.shape)],
        whole_spec((shard, plan.ffn)),
        shape_of((shard, plan.ffn), BF16),
        sc,
        [up_weight],
        "slice_up",
    )
    down_piece = jnp.concatenate(
        [
            lax.dynamic_slice_in_dim(down_weight, me * units, units, 0),
            lax.dynamic_slice_in_dim(up_bias, me * units, units, 0)[:, None],
        ],
        axis=1,
    )
    down_piece = jnp.pad(down_piece, ((0, 0), (0, up_to_lanes(width + 1) - width - 1)))

    def gather(piece, long_ahead):
        if plan.rings:
            return ring_gather(piece, wsh, long_ahead)
        return [lax.all_gather(piece, "wsh", axis=0, tiled=True)], [0]

    firsts, first_distances = gather(first_piece, True)
    x = ctx_gather(layer_input, ctx)
    cot = ctx_gather(output_cotangent, ctx)
    ups, up_distances = gather(up_piece, False)
    downs, down_distances = gather(down_piece, True)

    places = jnp.array([reverse_bits(p, ctx) for p in range(ctx)], jnp.int32)
    table = ((me ^ places)[:, None] * 2 + jnp.arange(2, dtype=jnp.int32)[None]).reshape(-1)
    blocks = jnp.arange(2 * ctx, dtype=jnp.int32)
    held = jnp.sum(jnp.where(table[:, None] == blocks[None], block_order[None], 0), axis=1)
    pos = (held[:, None] * half_block + jnp.arange(half_block, dtype=jnp.int32)[None]).reshape(-1)
    seg_blocks = segment_ids.reshape(seqs, 1, 2 * ctx, half_block)
    seg = jnp.sum(
        jnp.where((held[:, None] == blocks[None])[None, :, :, None], seg_blocks, 0), axis=2
    ).reshape(seqs, -1)

    first_in, projected, qkv_full, out_part, vec = project(plan, sc, x, firsts, first_distances)
    outs = ctx_gather(out_part, ctx)
    attended_own, weights = attend(plan, projected, pos, seg)
    att = ctx_gather(attended_own, ctx)

    odd = feed(plan, sc, 1, x, cot, vec, att, (outs, ups, up_distances, downs, down_distances), None)
    odd_part, odd_back, act, up_grad, second_in, attended, odd_sums, odd_bias = odd[:8]
    feed_weights = odd[8:]
    out_w = feed_weights[0]
    even = feed(plan, sc, 0, x, cot, vec, att, feed_weights, (act, up_grad, second_in, attended))
    even_part, even_back, act, up_grad, second_in, attended, even_sums, even_bias, resid = even

    odd_arrived = flip(fold(odd_back, ctx, last).astype(BF16), ctx, last)
    even_sum = fold(even_back, ctx, last).astype(F32)
    cot_own = output_cotangent.reshape(own, width)
    branch_own, resid_grad, second_sums = own_blocks(
        plan,
        functools.partial(second_kernel, plan),
        sc,
        (even_sum, odd_arrived, cot_own, resid),
        (vec,),
        (BF16, F32),
        ((VECTORS, width),),
        "second_back",
    )
    branch = ctx_gather(branch_own.reshape(seqs, rows, width), ctx)

    tokens = ctx * own
    down_grad = dot_cols(act.reshape(tokens, plan.ffn), cot.reshape(tokens, width))
    up_w_grad = dot_cols(second_in.reshape(tokens, width), up_grad.reshape(tokens, plan.ffn))
    up_b_grad = (odd_bias + even_bias).reshape(plan.ffn, 1)

    def scatter(parts, places, rows_out, wide, name, long_ahead):
        if plan.rings:
            return ring_scatter(
                functools.partial(step_sum, sc, parts, places, rows_out, wide, name), wsh, long_ahead
            )
        padded = jnp.zeros((rows_out * wsh, wide), BF16)
        for part, (at, count) in zip(parts, places, strict=True):
            padded = lax.dynamic_update_slice(padded, part[:, :count].astype(BF16), (0, at))
        return lax.psum_scatter(padded, "wsh", scatter_dimension=0, tiled=True)

    if plan.rings:
        ffn_sum = scatter(
            (up_w_grad, down_grad, up_b_grad),
            ((0, plan.ffn), (plan.down_at, width), (plan.bias_at, 1)),
            shard,
            plan.bias_at + 1,
            "ffn_step",
            True,
        )
        ffn_all = ctx_gather(ffn_sum, ctx)
        up_out, down_out, up_b_out = spread_out(
            plan,
            ffn_out_kernel,
            sc,
            ffn_all,
            ((shard, plan.hidden * wsh), (plan.hidden, width), (1, plan.hidden)),
            "ffn_out",
        )
    else:
        up_sum = lax.psum_scatter(up_w_grad.astype(BF16), "wsh", scatter_dimension=0, tiled=True)
        down_sum = lax.psum_scatter(
            jnp.concatenate([down_grad, up_b_grad], axis=1).astype(BF16),
            "wsh",
            scatter_dimension=0,
            tiled=True,
        )
        up_all = lax.all_gather(up_sum, "ctx", axis=0)
        up_out = jnp.transpose(up_all.reshape(ctx, shard, wsh, units), (1, 2, 0, 3))
        up_out = up_out.reshape(shard, plan.hidden * wsh).astype(F32)
        down_all = lax.all_gather(down_sum, "ctx", axis=0, tiled=True).astype(F32)
        down_out, up_b_out = down_all[:, :width], down_all[:, width]

    qkv_grad = attend_back(plan, sc, projected, weights, branch, out_w)
    first_part, small = first_back(
        plan, sc, qkv_grad, x, qkv_full, second_sums, odd_sums, even_sums
    )
    qkv_w_grad = dot_cols(first_in, qkv_grad.reshape(tokens, 3 * span))
    first_col = ((me * HEADS) // ctx) * HEAD_DIM
    out_w_grad = dot_cols(
        attended.reshape(tokens, width),
        lax.dynamic_slice_in_dim(branch.reshape(tokens, width), first_col, span, 1),
    )
    attn_sum = scatter(
        (qkv_w_grad, small, out_w_grad),
        ((0, 3 * span), (plan.vec_at, VECTORS), (plan.out_at, span)),
        shard,
        plan.first_wide,
        "attn_step",
        False,
    )
    attn_all = ctx_gather(attn_sum, ctx)
    qkv_out, out_out, small_out = spread_out(
        plan,
        attn_out_kernel,
        sc,
        attn_all,
        ((shard, 3 * width), (shard, width), (VECTORS, shard)),
        "attn_out",
    )

    kept = first_part
    bit = 1
    while bit < last:
        half = kept.shape[0] // 2
        kept = add_low(kept[:half], flip(kept[half:].astype(BF16), ctx, bit))
        bit *= 2
    (input_grad,) = own_blocks(
        plan,
        functools.partial(first_kernel, plan),
        sc,
        (
            kept[0].astype(F32),
            flip(kept[1].astype(BF16), ctx, last),
            layer_input.reshape(own, width),
            resid_grad,
        ),
        (vec,),
        (BF16,),
        (),
        "first_norm",
    )

    odd_out = flip(fold(odd_part, ctx, last).astype(BF16), ctx, last)
    even_out = fold(even_part, ctx, last)
    layer_out = (resid + add_low(even_out, odd_out) + vec[7]).astype(BF16)
    return (
        layer_out.reshape(layer_input.shape),
        input_grad.reshape(layer_input.shape),
        small_out[0],
        small_out[1],
        qkv_out,
        small_out[2:4],
        out_out,
        small_out[4],
        small_out[5],
        small_out[6],
        up_out,
        up_b_out.reshape(-1),
        down_out,
        small_out[7],
    )


def solution(mesh):
    token_spec = P("wsh", "ctx", None)
    vector = P("wsh")
    matrix = P("wsh", None)
    pair = P(None, "wsh")
    return jax.shard_map(
        per_device,
        mesh=mesh,
        in_specs=(
            token_spec,
            P("wsh", None),
            P(),
            vector,
            vector,
            matrix,
            pair,
            matrix,
            vector,
            vector,
            vector,
            matrix,
            vector,
            matrix,
            vector,
            token_spec,
        ),
        out_specs=(
            token_spec,
            token_spec,
            vector,
            vector,
            matrix,
            pair,
            matrix,
            vector,
            vector,
            vector,
            matrix,
            vector,
            matrix,
            vector,
        ),
        check_vma=False,
    )
```
